32 devices in a mesh: scan: 2 (over y), tile: 4 (over z), head: 4 (over x, core).
Axes of the slice: x: 2, y: 2, z: 4, core: 2. Of those that a mesh axis runs over, the one named last changes fastest.
Arguments:
- tiles: bfloat16 [4096, 1152], P(('scan', 'tile')), parts along dimension 0, may hold values from -6 to 6
- queries: bfloat16 [512, 4096], P(None, 'head'), may hold values from -41 to 41
- grad_out: bfloat16 [1024, 4096], P('scan', 'head'), parts along dimension 0, may hold values from -6 to 6
- key_weight: bfloat16 [1152, 4096], P('tile', 'head'), may hold values from -0.1875 to 0.1875
- value_weight: bfloat16 [1152, 4096], P('tile', 'head'), may hold values from -0.1875 to 0.1875
Outputs:
- grad_queries: bfloat16 [1024, 4096], P(('scan', 'tile'), 'head'), parts along dimension 0
- grad_key_weight: bfloat16 [2304, 4096], P(('scan', 'tile'), 'head'), parts along dimension 0
- grad_value_weight: bfloat16 [2304, 4096], P(('scan', 'tile'), 'head'), parts along dimension 0
- grad_tiles: bfloat16 [4096, 1152], P(('scan', 'tile'), 'head'), parts along dimension 0
The draws below stay inside these ranges and needn't reach their ends.
There are 2 independent parts, one for each index of `scan`. The reference program is written for one: setup_inputs(seed, part) draws one part's arguments, and reference() takes and returns one part's arrays. A program takes and returns all parts, laid end to end along the dimension named above; an argument that names none is the same for every part. Nothing has to cross between parts.
All inputs are finite; a program needn't handle non-finite values.
Results may differ from the reference program's by a relative error of at most 0.025.
The reference program's roundings to bfloat16 on the way (of `probs_b` and `dscores`) count: a program that leaves them out, or rounds other values in their place, can miss the bound.
Values may be sent and summed in bfloat16 or wider, within the bound.
A program may use at most 128 MiB of HBM per device.

```python
import jax
import jax.numpy as jnp
from jax import lax

NQ = 512
HEADS = 32
HD = 128
DX = 1152
TOK_DEV = 512
DM = 4096
TOKENS = 2048
N_TILE = 4
N_HEAD = 4


def draw_queries(key, part):
    second = jax.random.fold_in(key, 1)
    values = jax.random.truncated_normal(second, -6.0, 6.0, (NQ, DM), jnp.float32)
    return values.astype(jnp.bfloat16)


def block_scale(own_key, dims, cuts, least, largest):
    def one(dim, parts):
        steps = jax.random.uniform(jax.random.fold_in(jax.random.fold_in(own_key, 6), dim), (parts,), jnp.float32, least / len(cuts), largest / len(cuts))
        return jnp.repeat(jnp.exp(steps), dims[dim] // parts).reshape((-1,) + (1,) * (len(dims) - dim - 1))

    factor_of = one(*cuts[0])
    for cut in cuts[1:]:
        factor_of = factor_of * one(*cut)
    return factor_of


def noise(own_key, extent, scale, bound, pieces=(), dtype=jnp.bfloat16):
    drawn = scale * jax.random.normal(own_key, extent, jnp.float32)
    if pieces:
        drawn = drawn * block_scale(own_key, extent, pieces, -0.22, 0.18)
    return jnp.clip(drawn, -bound, bound).astype(dtype)


def setup_inputs(seed: int = 0, part: int = 0) -> dict:
    key_of = jax.random.split(jax.random.key(seed), 6)
    part_keys = jax.random.split(jax.random.fold_in(key_of[5], part), 6)
    tiles = noise(part_keys[0], (TOKENS, DX), 1.0, 6.0, ((0, 4),))
    queries = draw_queries(jax.random.fold_in(key_of[5], 71), part)
    grad_out = noise(part_keys[2], (NQ, DM), 1.0, 6.0, ((1, 4),))
    key_weight = noise(key_of[3], (DX, DM), DX ** -0.5, 0.1875, ((0, 4), (1, 4)))
    value_weight = noise(key_of[4], (DX, DM), DX ** -0.5, 0.1875, ((0, 4), (1, 4)))
    return dict(tiles=tiles, queries=queries, grad_out=grad_out, key_weight=key_weight, value_weight=value_weight)


def reference(tiles, queries, grad_out, key_weight, value_weight):
    groups = N_HEAD
    per = HEADS // groups
    width = per * HD
    scale = HD ** -0.5
    q_all = jnp.transpose(queries.reshape(NQ, groups, width), (1, 0, 2))
    d_all = jnp.transpose(grad_out.reshape(NQ, groups, width), (1, 0, 2))
    wk_all = jnp.transpose(key_weight.reshape(DX, groups, width), (1, 0, 2))
    wv_all = jnp.transpose(value_weight.reshape(DX, groups, width), (1, 0, 2))
    tiles_f = tiles.astype(jnp.float32)
    tiles_blocks = tiles_f.reshape(N_TILE, TOK_DEV, DX)

    def one_group(carry, items):
        qg, dg, wkg, wvg = items
        keys = jnp.dot(tiles, wkg, preferred_element_type=jnp.float32).astype(jnp.bfloat16)
        values = jnp.dot(tiles, wvg, preferred_element_type=jnp.float32).astype(jnp.bfloat16)
        kh = keys.astype(jnp.float32).reshape(TOKENS, per, HD)
        vh = values.astype(jnp.float32).reshape(TOKENS, per, HD)
        qh = qg.astype(jnp.float32).reshape(NQ, per, HD)
        dh = dg.astype(jnp.float32).reshape(NQ, per, HD)
        scores = jnp.einsum('qgd,tgd->gqt', qh, kh) * scale
        top = jnp.max(scores, axis=-1, keepdims=True)
        expo = jnp.exp(scores - top)
        probs = expo / jnp.sum(expo, axis=-1, keepdims=True)
        probs_b = probs.astype(jnp.bfloat16).astype(jnp.float32)
        attn = jnp.einsum('gqt,tgd->qgd', probs_b, vh)
        delta = jnp.transpose(jnp.sum(dh * attn, axis=-1), (1, 0))
        dprobs = jnp.einsum('qgd,tgd->gqt', dh, vh)
        dscores = (probs * (dprobs - delta[:, :, None]) * scale).astype(jnp.bfloat16).astype(jnp.float32)
        ds_blocks = dscores.reshape(per, NQ, N_TILE, TOK_DEV)
        k_blocks = kh.reshape(N_TILE, TOK_DEV, per, HD)
        dq_parts = jnp.einsum('gqnt,ntgd->nqgd', ds_blocks, k_blocks).astype(jnp.bfloat16).astype(jnp.float32)
        dq = jnp.sum(dq_parts, axis=0).reshape(NQ, width).astype(jnp.bfloat16)
        dkeys = jnp.einsum('gqt,qgd->tgd', dscores, qh).astype(jnp.bfloat16).reshape(TOKENS, width)
        dvalues = jnp.einsum('gqt,qgd->tgd', probs_b, dh).astype(jnp.bfloat16).reshape(TOKENS, width)
        dk_blocks = dkeys.astype(jnp.float32).reshape(N_TILE, TOK_DEV, width)
        dv_blocks = dvalues.astype(jnp.float32).reshape(N_TILE, TOK_DEV, width)
        gwk = jnp.sum(jnp.einsum('ntx,ntc->nxc', tiles_blocks, dk_blocks).astype(jnp.bfloat16).astype(jnp.float32), axis=0).astype(jnp.bfloat16)
        gwv = jnp.sum(jnp.einsum('ntx,ntc->nxc', tiles_blocks, dv_blocks).astype(jnp.bfloat16).astype(jnp.float32), axis=0).astype(jnp.bfloat16)
        term = jnp.einsum('tc,xc->tx', dkeys.astype(jnp.float32), wkg.astype(jnp.float32))
        term = term + jnp.einsum('tc,xc->tx', dvalues.astype(jnp.float32), wvg.astype(jnp.float32))
        carry = carry + term.astype(jnp.bfloat16).astype(jnp.float32)
        return carry, (dq, gwk, gwv)

    start = jnp.zeros((TOKENS, DX), jnp.float32)
    total, (dq_g, gwk_g, gwv_g) = lax.scan(one_group, start, (q_all, d_all, wk_all, wv_all))
    grad_queries = jnp.transpose(dq_g, (1, 0, 2)).reshape(NQ, DM)
    grad_key_weight = jnp.transpose(gwk_g, (1, 0, 2)).reshape(DX, DM)
    grad_value_weight = jnp.transpose(gwv_g, (1, 0, 2)).reshape(DX, DM)
    return grad_queries, grad_key_weight, grad_value_weight, total.astype(jnp.bfloat16)
```

```python
import functools

import jax
import jax.numpy as jnp
from jax import lax
from jax.experimental import pallas as pl
from jax.experimental.pallas import tpu as pltpu
from jax.sharding import PartitionSpec as P

HD = 128
MESH = pl.DeviceIdType.MESH
F32 = jnp.float32
BF16 = jnp.bfloat16


def combined_all(part, axis, combine):
    gathered = jax.tree.map(lambda a: lax.all_gather(a, axis), part)

    def take(source):
        return jax.tree.map(lambda a: lax.dynamic_index_in_dim(a, source, 0, False), gathered)

    return lax.fori_loop(
        1, lax.axis_size(axis), lambda source, state: combine(state, take(source)), take(0)
    )


def merge_pair(first, second):
    top = jnp.maximum(first[0], second[0])
    fa = jnp.exp(first[0] - top)
    fb = jnp.exp(second[0] - top)
    return (top, first[1] * fa + second[1] * fb)


def general_body(tiles, queries, grad_out, key_weight, value_weight):
    scale = HD ** (-0.5)
    tok_rows = tiles.shape[0]
    lat_rows = queries.shape[0]
    width = queries.shape[1]
    per = width // HD
    tile_count = lax.axis_size("tile")
    key_full, value_full = (
        lax.all_gather(key_weight, "tile", axis=0, tiled=True),
        lax.all_gather(value_weight, "tile", axis=0, tiled=True),
    )
    keys = jnp.dot(tiles, key_full, preferred_element_type=jnp.float32).astype(jnp.bfloat16)
    values = jnp.dot(tiles, value_full, preferred_element_type=jnp.float32).astype(jnp.bfloat16)
    key_heads = keys.reshape(tok_rows, per, HD)
    value_heads = values.reshape(tok_rows, per, HD)
    query_heads = queries.reshape(lat_rows, per, HD)
    cotangent = grad_out.reshape(lat_rows, per, HD)
    scores = (
        jnp.einsum("qgd,tgd->gqt", query_heads, key_heads, preferred_element_type=jnp.float32)
        * scale
    )
    local_top = jnp.max(scores, axis=-1)
    expo = jnp.exp(scores - local_top[:, :, None])
    local_total = jnp.sum(expo, axis=-1)
    dprobs = jnp.einsum("qgd,tgd->gqt", cotangent, value_heads, preferred_element_type=jnp.float32)
    top, total = combined_all((local_top, local_total), "tile", merge_pair)
    probs = expo * (jnp.exp(local_top - top) / total)[:, :, None]
    probs_b = probs.astype(jnp.bfloat16)
    attn_part = jnp.einsum("gqt,tgd->qgd", probs_b, value_heads, preferred_element_type=jnp.float32)
    attn = lax.psum(attn_part.astype(jnp.bfloat16), "tile").astype(jnp.float32)
    delta = jnp.transpose(jnp.sum(cotangent.astype(jnp.float32) * attn, axis=-1), (1, 0))
    dscores = (probs * (dprobs - delta[:, :, None]) * scale).astype(jnp.bfloat16)
    dkeys = jnp.einsum(
        "gqt,qgd->tgd", dscores, query_heads, preferred_element_type=jnp.float32
    ).astype(jnp.bfloat16)
    dvalues = jnp.einsum(
        "gqt,qgd->tgd", probs_b, cotangent, preferred_element_type=jnp.float32
    ).astype(jnp.bfloat16)
    kv_grad = jnp.concatenate(
        [dkeys.reshape(tok_rows, width), dvalues.reshape(tok_rows, width)], axis=1
    )
    lat_share = lat_rows // tile_count
    block = dscores
    grad_queries = lax.psum_scatter(
        jnp.einsum("gqt,tgd->qgd", block, key_heads, preferred_element_type=jnp.float32)
        .reshape(lat_share * lax.axis_size("tile"), width)
        .astype(jnp.bfloat16),
        "tile",
        scatter_dimension=0,
        tiled=True,
    )
    block = tiles
    both_grads = lax.psum_scatter(
        jnp.einsum("tx,tc->xc", block, kv_grad, preferred_element_type=jnp.float32).astype(
            jnp.bfloat16
        ),
        "tile",
        scatter_dimension=0,
        tiled=True,
    ).astype(jnp.float32)
    grad_key_weight = both_grads[:, :width].astype(jnp.bfloat16)
    grad_value_weight = both_grads[:, width:].astype(jnp.bfloat16)
    stacked = jnp.concatenate([key_full, value_full], axis=1)
    input_term = jnp.einsum("tc,xc->tx", kv_grad, stacked, preferred_element_type=jnp.float32)
    input_term = input_term.astype(jnp.bfloat16).astype(jnp.float32)
    grad_tiles = lax.psum_scatter(
        input_term.astype(jnp.bfloat16), "head", scatter_dimension=1, tiled=True
    )
    return (grad_queries, grad_key_weight, grad_value_weight, grad_tiles)


def dot_nn(a, b):
    return lax.dot_general(a, b, (((1,), (0,)), ((), ())), preferred_element_type=F32)


def dot_nt(a, b):
    return lax.dot_general(a, b, (((1,), (1,)), ((), ())), preferred_element_type=F32)


def dot_tn(a, b):
    return lax.dot_general(a, b, (((0,), (0,)), ((), ())), preferred_element_type=F32)


def kernel(
    tiles, queries, grad_out, key_weight, value_weight,
    gq_out, gwk_out, gwv_out, gt_out,
    tf, wc, qs, gs, kv, sc, dp, pb, ds, dkv, acc, dq_acc, gq_buf, gw_buf,
    part, rec_core, snd_x, rec_x, snd_z, rec_z, top, total, delta,
    loc_sem, out_sem,
    wz_send, wz_recv, wy_send, wy_recv,
    tz_send, tz_recv, tx_send, tx_recv, tc_send, tc_recv, td_send, td_recv,
    gq_send, gq_recv, gw_send, gw_recv,
    pc_send, pc_recv, px_send, px_recv, pz_send, pz_recv,
    *, count, mine,
):
    scale = HD ** (-0.5)
    scan, t, h = lax.axis_index("scan"), lax.axis_index("tile"), lax.axis_index("head")
    core, chip = lax.rem(h, 2), lax.div(h, 2)
    core_peer = {"head": h + 1 - 2 * core}
    chip_peer = {"head": h + 2 - 4 * chip}
    scan_peer = {"scan": 1 - scan}
    tok = tiles.shape[0]
    lat = queries.shape[0]
    cols = mine * HD
    wrow = key_weight.shape[0]
    half = wrow // 2
    quarter = tok // 4
    lat_own = lat // count
    peers = range(1, count)

    def ahead(k):
        return lax.rem(t + k, count)

    def behind(k):
        return lax.rem(t + count - k, count)

    def at_lanes(index, size):
        return pl.ds(pl.multiple_of(index * size, size), size)

    def rows(start, size, unit):
        return pl.ds(pl.multiple_of(start, unit), size)

    barrier = pltpu.get_barrier_semaphore()
    for k in peers:
        pl.semaphore_signal(barrier, inc=1, device_id={"tile": ahead(k)}, device_id_type=MESH)
    for peer in (core_peer, chip_peer, scan_peer):
        pl.semaphore_signal(barrier, inc=1, device_id=peer, device_id_type=MESH)
    pl.semaphore_wait(barrier, count - 1 + 3)

    def remote(src, dst, send, recv, peer):
        return pltpu.make_async_remote_copy(
            src_ref=src, dst_ref=dst, send_sem=send, recv_sem=recv,
            device_id=peer, device_id_type=MESH,
        )

    def w_send(k, which):
        to = ahead(k)
        src = (key_weight, value_weight)[which].at[rows(scan * half, half, 16), at_lanes(to, cols)]
        dst = wc.at[rows(t * wrow + scan * half, half, 16), pl.ds(which * cols, cols)]
        return remote(src, dst, wz_send.at[which, k - 1], wz_recv.at[which, k - 1], {"tile": to})

    def w_got(k, which):
        piece = wc.at[rows(behind(k) * wrow + scan * half, half, 16), pl.ds(which * cols, cols)]
        return remote(piece, piece, wz_send.at[which, k - 1], wz_recv.at[which, k - 1], scan_peer)

    def w_pass(k):
        piece = wc.at[rows(behind(k) * wrow + scan * half, half, 16), :]
        return remote(piece, piece, wy_send.at[k - 1], wy_recv.at[k - 1], scan_peer)

    def w_passed(k):
        piece = wc.at[rows(behind(k) * wrow + (1 - scan) * half, half, 16), :]
        return remote(piece, piece, wy_send.at[k - 1], wy_recv.at[k - 1], scan_peer)

    def t_piece(source, who):
        return tf.at[rows(source * tok + who * quarter, quarter, 16), :]

    def t_send(k):
        return remote(
            tiles.at[rows(h * quarter, quarter, 16), :], t_piece(t, h),
            tz_send.at[k - 1], tz_recv.at[k - 1], {"tile": ahead(k)},
        )

    def t_move(k, who, send, recv, peer):
        piece = t_piece(behind(k), who)
        return remote(piece, piece, send.at[k - 1], recv.at[k - 1], peer)

    h_core, h_chip = h + 1 - 2 * core, h + 2 - 4 * chip
    h_diag = h_chip + 1 - 2 * core

    for k in peers:
        for which in range(2):
            w_send(k, which).start()
    for k in peers:
        t_send(k).start()
    local = [
        pltpu.make_async_copy(tiles, tf.at[rows(t * tok, tok, 16), :], loc_sem.at[0]),
        pltpu.make_async_copy(
            key_weight.at[:, at_lanes(t, cols)], wc.at[rows(t * wrow, wrow, 16), pl.ds(0, cols)],
            loc_sem.at[1],
        ),
        pltpu.make_async_copy(
            value_weight.at[:, at_lanes(t, cols)],
            wc.at[rows(t * wrow, wrow, 16), pl.ds(cols, cols)], loc_sem.at[2],
        ),
        pltpu.make_async_copy(queries.at[:, at_lanes(t, cols)], qs, loc_sem.at[3]),
        pltpu.make_async_copy(grad_out.at[:, at_lanes(t, cols)], gs, loc_sem.at[4]),
    ]
    for copy in local:
        copy.start()
    for k in peers:
        for which in range(2):
            w_got(k, which).wait_recv()
        w_pass(k).start()
    top[...] = jnp.full_like(top, -jnp.inf)
    for copy in local:
        copy.wait()
    for k in peers:
        w_passed(k).wait_recv()

    SUB = 256

    def project(block):
        def sub(i, carry):
            at = rows(block * tok + i * SUB, SUB, SUB)
            kv[at, :] = dot_nn(tf[at, :], wc[...]).astype(BF16)
            for m in range(mine):
                lanes = slice(m * HD, (m + 1) * HD)
                vlanes = slice(cols + m * HD, cols + (m + 1) * HD)
                score = dot_nt(kv[at, lanes], qs[:, lanes]) * scale
                sc[m, at, :] = score
                top[m, :, :] = jnp.maximum(top[m, :, :], jnp.max(score, axis=0, keepdims=True))
                dp[m, at, :] = dot_nt(kv[at, vlanes], gs[:, lanes])
            return carry

        lax.fori_loop(0, tok // SUB, sub, 0)

    project(t)
    for k in peers:
        t_move(k, h, tz_send, tz_recv, core_peer).wait_recv()
        t_move(k, h, tx_send, tx_recv, chip_peer).start()
        t_move(k, h, tc_send, tc_recv, core_peer).start()
    for k in peers:
        t_move(k, h_chip, tx_send, tx_recv, chip_peer).wait_recv()
        t_move(k, h_chip, td_send, td_recv, core_peer).start()
    for k in peers:
        t_move(k, h_core, tc_send, tc_recv, core_peer).wait_recv()
        t_move(k, h_diag, td_send, td_recv, core_peer).wait_recv()
        project(behind(k))

    total[...] = jnp.zeros_like(total)

    EL = 128

    def exps(i, carry):
        at = rows(i * EL, EL, EL)
        for m in range(mine):
            expo = jnp.exp(sc[m, at, :] - top[m, :, :])
            sc[m, at, :] = expo
            total[m, :, :] = total[m, :, :] + jnp.sum(expo, axis=0, keepdims=True)
        return carry

    lax.fori_loop(0, count * tok // EL, exps, 0)
    total[...] = 1.0 / total[...]
    delta[...] = jnp.zeros_like(delta)

    def probs(i, carry):
        at = rows(i * EL, EL, EL)
        for m in range(mine):
            prob = sc[m, at, :] * total[m, :, :]
            prob_b = prob.astype(BF16)
            sc[m, at, :] = prob
            pb[m, at, :] = prob_b
            delta[m, :, :] = delta[m, :, :] + jnp.sum(
                prob_b.astype(F32) * dp[m, at, :], axis=0, keepdims=True
            )
        return carry

    lax.fori_loop(0, count * tok // EL, probs, 0)

    def weight_grad(lo):
        acc[...] = jnp.zeros_like(acc)

        def block(b, carry):
            at = rows(b * tok, tok, tok)
            term = dot_tn(dkv[at, lo : lo + cols], tf[at, :])
            acc[...] += term.astype(BF16).astype(F32)
            return carry

        lax.fori_loop(0, count, block, 0)
        gw_buf[:, lo : lo + cols] = jnp.transpose(acc[...], (1, 0)).astype(BF16)

    def gw_own(which):
        out = (gwk_out, gwv_out)[which]
        return pltpu.make_async_copy(
            gw_buf.at[rows(t * wrow, wrow, 16), pl.ds(which * cols, cols)],
            out.at[:, at_lanes(t, cols)], out_sem.at[which],
        )

    def gw_move(k, which):
        out = (gwk_out, gwv_out)[which]
        to = ahead(k)
        return remote(
            gw_buf.at[rows(to * wrow, wrow, 16), pl.ds(which * cols, cols)],
            out.at[:, at_lanes(t, cols)],
            gw_send.at[which, k - 1], gw_recv.at[which, k - 1], {"tile": to},
        )

    def gw_got(k, which):
        out = (gwk_out, gwv_out)[which]
        return remote(
            gw_buf.at[rows(t * wrow, wrow, 16), pl.ds(which * cols, cols)],
            out.at[:, at_lanes(behind(k), cols)],
            gw_send.at[which, k - 1], gw_recv.at[which, k - 1], {"tile": ahead(k)},
        )

    def dvals(b, carry):
        at = rows(b * tok, tok, tok)
        for m in range(mine):
            lanes = slice(m * HD, (m + 1) * HD)
            dkv[at, cols + m * HD : cols + (m + 1) * HD] = dot_nn(
                pb[m, at, :], gs[:, lanes]
            ).astype(BF16)
        return carry

    lax.fori_loop(0, count, dvals, 0)
    weight_grad(cols)
    for k in peers:
        gw_move(k, 1).start()
    gw_own(1).start()

    dq_acc[...] = jnp.zeros_like(dq_acc)

    def part_core(b):
        return remote(
            part.at[1 - core, b], rec_core.at[b], pc_send.at[b], pc_recv.at[b], core_peer
        )

    xrow = tiles.shape[1] // 4

    def grads(j, carry):
        b = lax.rem(t + 1 + j, count)
        at = rows(b * tok, tok, tok)
        for m in range(mine):
            lanes = slice(m * HD, (m + 1) * HD)

            def sub(i, carry):
                sub_at = rows(b * tok + i * EL, EL, EL)
                ds[pl.ds(pl.multiple_of(i * EL, EL), EL), :] = (
                    sc[m, sub_at, :] * (dp[m, sub_at, :] - delta[m, :, :]) * scale
                ).astype(BF16)
                return carry

            lax.fori_loop(0, tok // EL, sub, 0)
            dkv[at, lanes] = dot_nn(ds[...], qs[:, lanes]).astype(BF16)
            dq_acc[lanes, :] += dot_tn(kv[at, lanes], ds[...]).astype(BF16).astype(F32)
        for group in range(4):
            part[group % 2, b, group // 2, :, :] = dot_nt(
                wc[group * xrow : (group + 1) * xrow, :], dkv[at, :]
            ).astype(BF16)
        part_core(b).start()
        return carry

    lax.fori_loop(0, count, grads, 0)
    gq_buf[...] = jnp.transpose(dq_acc[...], (1, 0)).astype(BF16)

    def gq_move(k):
        return remote(
            gq_buf.at[rows(ahead(k) * lat_own, lat_own, 16), :], gq_out.at[:, at_lanes(t, cols)],
            gq_send.at[k - 1], gq_recv.at[k - 1], {"tile": ahead(k)},
        )

    def gq_got(k):
        return remote(
            gq_buf.at[rows(t * lat_own, lat_own, 16), :],
            gq_out.at[:, at_lanes(behind(k), cols)],
            gq_send.at[k - 1], gq_recv.at[k - 1], {"tile": ahead(k)},
        )

    gq_own = pltpu.make_async_copy(
        gq_buf.at[rows(t * lat_own, lat_own, 16), :], gq_out.at[:, at_lanes(t, cols)],
        out_sem.at[2],
    )

    def part_chip(b):
        return remote(snd_x.at[b], rec_x.at[b], px_send.at[b], px_recv.at[b], chip_peer)

    def to_chip(j, carry):
        b = lax.rem(t + 1 + j, count)
        part_core(b).wait_recv()
        snd_x[b, :, :] = (
            part[core, b, 1 - chip, :, :].astype(F32) + rec_core[b, 1 - chip, :, :].astype(F32)
        ).astype(BF16)
        part_chip(b).start()
        return carry

    lax.fori_loop(0, count, to_chip, 0)
    for k in peers:
        gq_move(k).start()
    gq_own.start()
    weight_grad(0)
    for k in peers:
        gw_move(k, 0).start()
    gw_own(0).start()

    def summed(b):
        return (
            part[core, b, chip, :, :].astype(F32)
            + rec_core[b, chip, :, :].astype(F32)
            + rec_x[b, :, :].astype(F32)
        )

    def part_tile(k):
        return remote(
            snd_z.at[k - 1], rec_z.at[k - 1], pz_send.at[k - 1], pz_recv.at[k - 1],
            {"tile": ahead(k)},
        )

    for k in peers:
        b = ahead(k)
        part_chip(b).wait_recv()
        snd_z[k - 1, :, :] = summed(b).astype(BF16)
        part_tile(k).start()
    part_chip(t).wait_recv()
    whole = summed(t)
    for k in peers:
        part_tile(k).wait_recv()
        whole = whole + rec_z[k - 1, :, :].astype(F32)
    gt_out[...] = jnp.transpose(whole, (1, 0)).astype(BF16)

    for k in peers:
        for which in range(2):
            w_send(k, which).wait_send()
            gw_got(k, which).wait_recv()
            gw_move(k, which).wait_send()
        w_pass(k).wait_send()
        t_send(k).wait_send()
        t_move(k, h, tx_send, tx_recv, chip_peer).wait_send()
        t_move(k, h, tc_send, tc_recv, core_peer).wait_send()
        t_move(k, h_chip, td_send, td_recv, core_peer).wait_send()
        gq_got(k).wait_recv()
        gq_move(k).wait_send()
        part_tile(k).wait_send()
    for j in range(count):
        part_core(j).wait_send()
        part_chip(j).wait_send()
    gq_own.wait()
    gw_own(0).wait()
    gw_own(1).wait()


def split_body(count, mine, tiles, queries, grad_out, key_weight, value_weight):
    tok, dx = tiles.shape
    lat, width = queries.shape
    wrow = key_weight.shape[0]
    cols = mine * HD
    tokens = tok * count
    xrow = dx // 4
    any_ = pl.BlockSpec(memory_space=pl.ANY)
    dma = pltpu.SemaphoreType.DMA
    peers = count - 1
    return pl.pallas_call(
        functools.partial(kernel, count=count, mine=mine),
        out_shape=(
            jax.ShapeDtypeStruct((lat // count, width), BF16),
            jax.ShapeDtypeStruct((wrow, width), BF16),
            jax.ShapeDtypeStruct((wrow, width), BF16),
            jax.ShapeDtypeStruct((tok, xrow), BF16),
        ),
        in_specs=[any_] * 5,
        out_specs=(any_, any_, any_, pl.BlockSpec(memory_space=pltpu.VMEM)),
        scratch_shapes=[
            pltpu.VMEM((tokens, dx), BF16),
            pltpu.VMEM((dx, 2 * cols), BF16),
            pltpu.VMEM((lat, cols), BF16),
            pltpu.VMEM((lat, cols), BF16),
            pltpu.VMEM((tokens, 2 * cols), BF16),
            pltpu.VMEM((mine, tokens, lat), F32),
            pltpu.VMEM((mine, tokens, lat), F32),
            pltpu.VMEM((mine, tokens, lat), BF16),
            pltpu.VMEM((tok, lat), BF16),
            pltpu.VMEM((tokens, 2 * cols), BF16),
            pltpu.VMEM((cols, dx), F32),
            pltpu.VMEM((cols, lat), F32),
            pltpu.VMEM((lat, cols), BF16),
            pltpu.VMEM((dx, 2 * cols), BF16),
            pltpu.VMEM((2, count, 2, xrow, tok), BF16),
            pltpu.VMEM((count, 2, xrow, tok), BF16),
            pltpu.VMEM((count, xrow, tok), BF16),
            pltpu.VMEM((count, xrow, tok), BF16),
            pltpu.VMEM((peers, xrow, tok), BF16),
            pltpu.VMEM((peers, xrow, tok), BF16),
            pltpu.VMEM((mine, 1, lat), F32),
            pltpu.VMEM((mine, 1, lat), F32),
            pltpu.VMEM((mine, 1, lat), F32),
            dma((5,)), dma((3,)),
            dma((2, peers)), dma((2, peers)), dma((peers,)), dma((peers,)),
            dma((peers,)), dma((peers,)), dma((peers,)), dma((peers,)),
            dma((peers,)), dma((peers,)), dma((peers,)), dma((peers,)),
            dma((peers,)), dma((peers,)), dma((2, peers)), dma((2, peers)),
            dma((count,)), dma((count,)), dma((count,)), dma((count,)),
            dma((peers,)), dma((peers,)),
        ],
        compiler_params=pltpu.CompilerParams(
            collective_id=0, has_side_effects=True, vmem_limit_bytes=60 * 1024 * 1024
        ),
    )(tiles, queries, grad_out, key_weight, value_weight)


def solution(mesh):
    count, groups = mesh.shape["tile"], mesh.shape["head"]

    def body(tiles, queries, grad_out, key_weight, value_weight):
        per = queries.shape[1] // HD
        split = (
            per % count == 0
            and groups == 4
            and mesh.shape["scan"] == 2
            and tiles.shape[0] % 512 == 0
            and tiles.shape[1] % 64 == 0
            and key_weight.shape[0] % 32 == 0
            and queries.shape[0] % (16 * count) == 0
        )
        chosen = functools.partial(split_body, count, per // count) if split else general_body
        return chosen(tiles, queries, grad_out, key_weight, value_weight)

    placed = (
        P(("scan", "tile"), None),
        P(None, "head"),
        P("scan", "head"),
        P("tile", "head"),
        P("tile", "head"),
    )
    return jax.shard_map(
        body,
        mesh=mesh,
        in_specs=placed,
        out_specs=(
            P(("scan", "tile"), "head"),
            P(("scan", "tile"), "head"),
            P(("scan", "tile"), "head"),
            P(("scan", "tile"), "head"),
        ),
        check_vma=False,
    )
```

```python
import functools

import jax
import jax.numpy as jnp
from jax import lax
from jax.experimental import pallas as pl
from jax.experimental.pallas import tpu as pltpu
from jax.sharding import PartitionSpec as P

HD = 128
MESH = pl.DeviceIdType.MESH
F32 = jnp.float32
BF16 = jnp.bfloat16


def combined_all(part, axis, combine):
    gathered = jax.tree.map(lambda a: lax.all_gather(a, axis), part)

    def take(source):
        return jax.tree.map(lambda a: lax.dynamic_index_in_dim(a, source, 0, False), gathered)

    return lax.fori_loop(
        1, lax.axis_size(axis), lambda source, state: combine(state, take(source)), take(0)
    )


def merge_pair(first, second):
    top = jnp.maximum(first[0], second[0])
    fa = jnp.exp(first[0] - top)
    fb = jnp.exp(second[0] - top)
    return (top, first[1] * fa + second[1] * fb)


def general_body(tiles, queries, grad_out, key_weight, value_weight):
    scale = HD ** (-0.5)
    tok_rows = tiles.shape[0]
    lat_rows = queries.shape[0]
    width = queries.shape[1]
    per = width // HD
    tile_count = lax.axis_size("tile")
    key_full, value_full = (
        lax.all_gather(key_weight, "tile", axis=0, tiled=True),
        lax.all_gather(value_weight, "tile", axis=0, tiled=True),
    )
    keys = jnp.dot(tiles, key_full, preferred_element_type=jnp.float32).astype(jnp.bfloat16)
    values = jnp.dot(tiles, value_full, preferred_element_type=jnp.float32).astype(jnp.bfloat16)
    key_heads = keys.reshape(tok_rows, per, HD)
    value_heads = values.reshape(tok_rows, per, HD)
    query_heads = queries.reshape(lat_rows, per, HD)
    cotangent = grad_out.reshape(lat_rows, per, HD)
    scores = (
        jnp.einsum("qgd,tgd->gqt", query_heads, key_heads, preferred_element_type=jnp.float32)
        * scale
    )
    local_top = jnp.max(scores, axis=-1)
    expo = jnp.exp(scores - local_top[:, :, None])
    local_total = jnp.sum(expo, axis=-1)
    dprobs = jnp.einsum("qgd,tgd->gqt", cotangent, value_heads, preferred_element_type=jnp.float32)
    top, total = combined_all((local_top, local_total), "tile", merge_pair)
    probs = expo * (jnp.exp(local_top - top) / total)[:, :, None]
    probs_b = probs.astype(jnp.bfloat16)
    attn_part = jnp.einsum("gqt,tgd->qgd", probs_b, value_heads, preferred_element_type=jnp.float32)
    attn = lax.psum(attn_part.astype(jnp.bfloat16), "tile").astype(jnp.float32)
    delta = jnp.transpose(jnp.sum(cotangent.astype(jnp.float32) * attn, axis=-1), (1, 0))
    dscores = (probs * (dprobs - delta[:, :, None]) * scale).astype(jnp.bfloat16)
    dkeys = jnp.einsum(
        "gqt,qgd->tgd", dscores, query_heads, preferred_element_type=jnp.float32
    ).astype(jnp.bfloat16)
    dvalues = jnp.einsum(
        "gqt,qgd->tgd", probs_b, cotangent, preferred_element_type=jnp.float32
    ).astype(jnp.bfloat16)
    kv_grad = jnp.concatenate(
        [dkeys.reshape(tok_rows, width), dvalues.reshape(tok_rows, width)], axis=1
    )
    lat_share = lat_rows // tile_count
    block = dscores
    grad_queries = lax.psum_scatter(
        jnp.einsum("gqt,tgd->qgd", block, key_heads, preferred_element_type=jnp.float32)
        .reshape(lat_share * lax.axis_size("tile"), width)
        .astype(jnp.bfloat16),
        "tile",
        scatter_dimension=0,
        tiled=True,
    )
    block = tiles
    both_grads = lax.psum_scatter(
        jnp.einsum("tx,tc->xc", block, kv_grad, preferred_element_type=jnp.float32).astype(
            jnp.bfloat16
        ),
        "tile",
        scatter_dimension=0,
        tiled=True,
    ).astype(jnp.float32)
    grad_key_weight = both_grads[:, :width].astype(jnp.bfloat16)
    grad_value_weight = both_grads[:, width:].astype(jnp.bfloat16)
    stacked = jnp.concatenate([key_full, value_full], axis=1)
    input_term = jnp.einsum("tc,xc->tx", kv_grad, stacked, preferred_element_type=jnp.float32)
    input_term = input_term.astype(jnp.bfloat16).astype(jnp.float32)
    grad_tiles = lax.psum_scatter(
        input_term.astype(jnp.bfloat16), "head", scatter_dimension=1, tiled=True
    )
    return (grad_queries, grad_key_weight, grad_value_weight, grad_tiles)


def dot_nn(a, b):
    return lax.dot_general(a, b, (((1,), (0,)), ((), ())), preferred_element_type=F32)


def dot_nt(a, b):
    return lax.dot_general(a, b, (((1,), (1,)), ((), ())), preferred_element_type=F32)


def dot_tn(a, b):
    return lax.dot_general(a, b, (((0,), (0,)), ((), ())), preferred_element_type=F32)


def kernel(
    tiles, queries, grad_out, key_weight, value_weight,
    gq_out, gwk_out, gwv_out, gt_out,
    tf, wc, qs, gs, kv, sc, dp, pb, ds, dkv, acc, dq_acc, gq_buf, gw_buf,
    part, rec_core, snd_x, rec_x, snd_z, rec_z, acc_t, top, total, delta,
    loc_sem, out_sem,
    wz_send, wz_recv, wy_send, wy_recv,
    tz_send, tz_recv, tx_send, tx_recv, tc_send, tc_recv, td_send, td_recv,
    gq_send, gq_recv, gw_send, gw_recv,
    pc_send, pc_recv, px_send, px_recv, pz_send, pz_recv,
    *, count, mine,
):
    scale = HD ** (-0.5)
    scan, t, h = lax.axis_index("scan"), lax.axis_index("tile"), lax.axis_index("head")
    core, chip = lax.rem(h, 2), lax.div(h, 2)
    core_peer = {"head": h + 1 - 2 * core}
    chip_peer = {"head": h + 2 - 4 * chip}
    scan_peer = {"scan": 1 - scan}
    tok = tiles.shape[0]
    lat = queries.shape[0]
    cols = mine * HD
    wrow = key_weight.shape[0]
    half = wrow // 2
    quarter = tok // 4
    lat_own = lat // count
    peers = range(1, count)

    def ahead(k):
        return lax.rem(t + k, count)

    def behind(k):
        return lax.rem(t + count - k, count)

    def at_lanes(index, size):
        return pl.ds(pl.multiple_of(index * size, size), size)

    def rows(start, size, unit):
        return pl.ds(pl.multiple_of(start, unit), size)

    barrier = pltpu.get_barrier_semaphore()
    for k in peers:
        pl.semaphore_signal(barrier, inc=1, device_id={"tile": ahead(k)}, device_id_type=MESH)
    for peer in (core_peer, chip_peer, scan_peer):
        pl.semaphore_signal(barrier, inc=1, device_id=peer, device_id_type=MESH)
    pl.semaphore_wait(barrier, count - 1 + 3)

    def remote(src, dst, send, recv, peer):
        return pltpu.make_async_remote_copy(
            src_ref=src, dst_ref=dst, send_sem=send, recv_sem=recv,
            device_id=peer, device_id_type=MESH,
        )

    def w_send(k, which):
        to = ahead(k)
        src = (key_weight, value_weight)[which].at[rows(scan * half, half, 16), at_lanes(to, cols)]
        dst = wc.at[rows(t * wrow + scan * half, half, 16), pl.ds(which * cols, cols)]
        return remote(src, dst, wz_send.at[which, k - 1], wz_recv.at[which, k - 1], {"tile": to})

    def w_got(k, which):
        piece = wc.at[rows(behind(k) * wrow + scan * half, half, 16), pl.ds(which * cols, cols)]
        return remote(piece, piece, wz_send.at[which, k - 1], wz_recv.at[which, k - 1], scan_peer)

    def w_pass(k):
        piece = wc.at[rows(behind(k) * wrow + scan * half, half, 16), :]
        return remote(piece, piece, wy_send.at[k - 1], wy_recv.at[k - 1], scan_peer)

    def w_passed(k):
        piece = wc.at[rows(behind(k) * wrow + (1 - scan) * half, half, 16), :]
        return remote(piece, piece, wy_send.at[k - 1], wy_recv.at[k - 1], scan_peer)

    def t_piece(source, who):
        return tf.at[rows(source * tok + who * quarter, quarter, 16), :]

    def t_hop(source, way):
        to = {"tile": lax.rem(t + count + 1 - 2 * way, count)}
        piece = t_piece(source, h)
        return remote(piece, piece, tz_send.at[way, source], tz_recv.at[source], to)

    def t_own(way):
        to = {"tile": lax.rem(t + count + 1 - 2 * way, count)}
        src = tiles.at[rows(h * quarter, quarter, 16), :]
        return remote(src, t_piece(t, h), tz_send.at[way, t], tz_recv.at[t], to)

    def t_move(source, who, send, recv, peer):
        piece = t_piece(source, who)
        return remote(piece, piece, send.at[source], recv.at[source], peer)

    inner = (t < count - 1, t > 0)

    def t_stage(j):
        for way, source, there in (
            (0, behind(j + 1), t - 1 - j >= 0),
            (1, ahead(j + 1), t + 1 + j < count),
        ):
            @pl.when(there)
            def _(way=way, source=source):
                t_move(source, h, tc_send, tz_recv, core_peer).wait_recv()

                @pl.when(inner[way])
                def _():
                    t_hop(source, way).start()

                t_move(source, h, tx_send, tx_recv, chip_peer).start()
                t_move(source, h, tc_send, tc_recv, core_peer).start()

    h_core, h_chip = h + 1 - 2 * core, h + 2 - 4 * chip
    h_diag = h_chip + 1 - 2 * core

    for way in range(2):
        @pl.when(inner[way])
        def _(way=way):
            t_own(way).start()

    for k in peers:
        for which in range(2):
            w_send(k, which).start()
    local = [
        pltpu.make_async_copy(tiles, tf.at[rows(t * tok, tok, 16), :], loc_sem.at[0]),
        pltpu.make_async_copy(
            key_weight.at[:, at_lanes(t, cols)], wc.at[rows(t * wrow, wrow, 16), pl.ds(0, cols)],
            loc_sem.at[1],
        ),
        pltpu.make_async_copy(
            value_weight.at[:, at_lanes(t, cols)],
            wc.at[rows(t * wrow, wrow, 16), pl.ds(cols, cols)], loc_sem.at[2],
        ),
        pltpu.make_async_copy(queries.at[:, at_lanes(t, cols)], qs, loc_sem.at[3]),
        pltpu.make_async_copy(grad_out.at[:, at_lanes(t, cols)], gs, loc_sem.at[4]),
    ]
    for copy in local:
        copy.start()
    t_stage(0)
    for k in peers:
        for which in range(2):
            w_got(k, which).wait_recv()
        w_pass(k).start()
    for j in range(1, count - 1):
        t_stage(j)
    top[...] = jnp.full_like(top, -jnp.inf)
    for copy in local:
        copy.wait()
    for k in peers:
        w_passed(k).wait_recv()

    SUB = 256

    def project(block):
        def sub(i, carry):
            at = rows(block * tok + i * SUB, SUB, SUB)
            kv[at, :] = dot_nn(tf[at, :], wc[...]).astype(BF16)
            for m in range(mine):
                lanes = slice(m * HD, (m + 1) * HD)
                vlanes = slice(cols + m * HD, cols + (m + 1) * HD)
                score = dot_nt(kv[at, lanes], qs[:, lanes]) * scale
                sc[m, at, :] = score
                top[m, :, :] = jnp.maximum(top[m, :, :], jnp.max(score, axis=0, keepdims=True))
                dp[m, at, :] = dot_nt(kv[at, vlanes], gs[:, lanes])
            return carry

        lax.fori_loop(0, tok // SUB, sub, 0)

    def chip_stage(j):
        for source, there in ((behind(j + 1), t - 1 - j >= 0), (ahead(j + 1), t + 1 + j < count)):
            @pl.when(there)
            def _(source=source):
                t_move(source, h_chip, tx_send, tx_recv, chip_peer).wait_recv()
                t_move(source, h_chip, td_send, td_recv, core_peer).start()

    def block_stage(j, carry):
        chip_stage(j)
        for source, there in (
            (lax.rem(t + count - 1 - j, count), t - 1 - j >= 0),
            (lax.rem(t + 1 + j, count), t + 1 + j < count),
        ):
            @pl.when(there)
            def _(source=source):
                t_move(source, h_core, tc_send, tc_recv, core_peer).wait_recv()
                t_move(source, h_diag, td_send, td_recv, core_peer).wait_recv()
                project(source)
        return carry

    project(t)
    lax.fori_loop(0, count - 1, block_stage, 0)

    total[...] = jnp.zeros_like(total)

    EL = 128

    def exps(i, carry):
        at = rows(i * EL, EL, EL)
        for m in range(mine):
            expo = jnp.exp(sc[m, at, :] - top[m, :, :])
            sc[m, at, :] = expo
            total[m, :, :] = total[m, :, :] + jnp.sum(expo, axis=0, keepdims=True)
        return carry

    lax.fori_loop(0, count * tok // EL, exps, 0)
    total[...] = 1.0 / total[...]
    delta[...] = jnp.zeros_like(delta)

    def probs(i, carry):
        at = rows(i * EL, EL, EL)
        for m in range(mine):
            prob = sc[m, at, :] * total[m, :, :]
            prob_b = prob.astype(BF16)
            sc[m, at, :] = prob
            pb[m, at, :] = prob_b
            delta[m, :, :] = delta[m, :, :] + jnp.sum(
                prob_b.astype(F32) * dp[m, at, :], axis=0, keepdims=True
            )
        return carry

    lax.fori_loop(0, count * tok // EL, probs, 0)

    def weight_grad(lo):
        acc[...] = jnp.zeros_like(acc)

        def block(b, carry):
            at = rows(b * tok, tok, tok)
            term = dot_tn(dkv[at, lo : lo + cols], tf[at, :])
            acc[...] += term.astype(BF16).astype(F32)
            return carry

        lax.fori_loop(0, count, block, 0)
        gw_buf[:, lo : lo + cols] = jnp.transpose(acc[...], (1, 0)).astype(BF16)

    def gw_own(which):
        out = (gwk_out, gwv_out)[which]
        return pltpu.make_async_copy(
            gw_buf.at[rows(t * wrow, wrow, 16), pl.ds(which * cols, cols)],
            out.at[:, at_lanes(t, cols)], out_sem.at[which],
        )

    def gw_move(k, which):
        out = (gwk_out, gwv_out)[which]
        to = ahead(k)
        return remote(
            gw_buf.at[rows(to * wrow, wrow, 16), pl.ds(which * cols, cols)],
            out.at[:, at_lanes(t, cols)],
            gw_send.at[which, k - 1], gw_recv.at[which, k - 1], {"tile": to},
        )

    def gw_got(k, which):
        out = (gwk_out, gwv_out)[which]
        return remote(
            gw_buf.at[rows(t * wrow, wrow, 16), pl.ds(which * cols, cols)],
            out.at[:, at_lanes(behind(k), cols)],
            gw_send.at[which, k - 1], gw_recv.at[which, k - 1], {"tile": ahead(k)},
        )

    def dvals(b, carry):
        at = rows(b * tok, tok, tok)
        for m in range(mine):
            lanes = slice(m * HD, (m + 1) * HD)
            dkv[at, cols + m * HD : cols + (m + 1) * HD] = dot_nn(
                pb[m, at, :], gs[:, lanes]
            ).astype(BF16)
        return carry

    lax.fori_loop(0, count, dvals, 0)
    weight_grad(cols)
    for k in peers:
        gw_move(k, 1).start()
    gw_own(1).start()

    dq_acc[...] = jnp.zeros_like(dq_acc)

    def part_core(b):
        return remote(
            part.at[1 - core, b], rec_core.at[b], pc_send.at[b], pc_recv.at[b], core_peer
        )

    xrow = tiles.shape[1] // 4

    def order(j):
        low = lax.rem(t, 2)
        high = lax.div(t, 2)
        first, second, third = 3 - 3 * high, 2 - 2 * low + high, 1 + low
        return jnp.where(j == 0, first, jnp.where(j == 1, second, jnp.where(j == 2, third, t)))

    def part_chip(b):
        return remote(snd_x.at[b], rec_x.at[b], px_send.at[b], px_recv.at[b], chip_peer)

    def to_chip(b):
        part_core(b).wait_recv()
        snd_x[b, :, :] = (
            part[core, b, 1 - chip, :, :].astype(F32) + rec_core[b, 1 - chip, :, :].astype(F32)
        ).astype(BF16)
        part_chip(b).start()

    def grads(j, carry):
        b = order(j)
        at = rows(b * tok, tok, tok)
        for m in range(mine):
            lanes = slice(m * HD, (m + 1) * HD)

            def sub(i, carry):
                sub_at = rows(b * tok + i * EL, EL, EL)
                ds[pl.ds(pl.multiple_of(i * EL, EL), EL), :] = (
                    sc[m, sub_at, :] * (dp[m, sub_at, :] - delta[m, :, :]) * scale
                ).astype(BF16)
                return carry

            lax.fori_loop(0, tok // EL, sub, 0)
            dkv[at, lanes] = dot_nn(ds[...], qs[:, lanes]).astype(BF16)
            dq_acc[lanes, :] += dot_tn(kv[at, lanes], ds[...]).astype(BF16).astype(F32)
        for group in range(4):
            part[group % 2, b, group // 2, :, :] = dot_nt(
                wc[group * xrow : (group + 1) * xrow, :], dkv[at, :]
            ).astype(BF16)
        part_core(b).start()

        @pl.when(j > 0)
        def _():
            to_chip(order(j - 1))

        return carry

    lax.fori_loop(0, count, grads, 0)
    to_chip(order(count - 1))
    gq_buf[...] = jnp.transpose(dq_acc[...], (1, 0)).astype(BF16)

    def gq_move(k):
        return remote(
            gq_buf.at[rows(ahead(k) * lat_own, lat_own, 16), :], gq_out.at[:, at_lanes(t, cols)],
            gq_send.at[k - 1], gq_recv.at[k - 1], {"tile": ahead(k)},
        )

    def gq_got(k):
        return remote(
            gq_buf.at[rows(t * lat_own, lat_own, 16), :],
            gq_out.at[:, at_lanes(behind(k), cols)],
            gq_send.at[k - 1], gq_recv.at[k - 1], {"tile": ahead(k)},
        )

    gq_own = pltpu.make_async_copy(
        gq_buf.at[rows(t * lat_own, lat_own, 16), :], gq_out.at[:, at_lanes(t, cols)],
        out_sem.at[2],
    )

    for k in peers:
        gq_move(k).start()
    gq_own.start()
    weight_grad(0)
    for k in peers:
        gw_move(k, 0).start()
    gw_own(0).start()

    def summed(b):
        return (
            part[core, b, chip, :, :].astype(F32)
            + rec_core[b, chip, :, :].astype(F32)
            + rec_x[b, :, :].astype(F32)
        )

    def part_tile(b, way):
        to = {"tile": lax.rem(t + count + 1 - 2 * way, count)}
        return remote(
            snd_z.at[b], rec_z.at[way, b], pz_send.at[b], pz_recv.at[way, b], to
        )

    for j in range(count - 1):
        b = order(j)
        part_chip(b).wait_recv()
        for way, onward, fed in ((0, b > t, t > 0), (1, b < t, t < count - 1)):
            @pl.when(onward)
            def _(way=way, fed=fed, b=b):
                @pl.when(fed)
                def _():
                    part_tile(b, way).wait_recv()
                    snd_z[b, :, :] = (summed(b) + rec_z[way, b, :, :].astype(F32)).astype(BF16)

                @pl.when(jnp.logical_not(fed))
                def _():
                    snd_z[b, :, :] = summed(b).astype(BF16)

                part_tile(b, way).start()

    part_chip(t).wait_recv()
    acc_t[...] = summed(t)
    for way, fed in ((0, t > 0), (1, t < count - 1)):
        @pl.when(fed)
        def _(way=way):
            part_tile(t, way).wait_recv()
            acc_t[...] += rec_z[way, t, :, :].astype(F32)

    gt_out[...] = jnp.transpose(acc_t[...], (1, 0)).astype(BF16)

    for k in peers:
        for which in range(2):
            w_send(k, which).wait_send()
            gw_got(k, which).wait_recv()
            gw_move(k, which).wait_send()
        w_pass(k).wait_send()
        source = behind(k)
        t_move(source, h, tx_send, tx_recv, chip_peer).wait_send()
        t_move(source, h, tc_send, tc_recv, core_peer).wait_send()
        t_move(source, h_chip, td_send, td_recv, core_peer).wait_send()
        gq_got(k).wait_recv()
        gq_move(k).wait_send()
        part_tile(behind(k), 0).wait_send()
    for way in range(2):
        @pl.when(inner[way])
        def _(way=way):
            t_own(way).wait_send()
            for j in range(count - 1):
                source = (behind, ahead)[way](j + 1)

                @pl.when((t - 1 - j >= 0, t + 1 + j < count)[way])
                def _():
                    t_hop(source, way).wait_send()

    for j in range(count):
        part_core(j).wait_send()
        part_chip(j).wait_send()
    gq_own.wait()
    gw_own(0).wait()
    gw_own(1).wait()


def split_body(count, mine, tiles, queries, grad_out, key_weight, value_weight):
    tok, dx = tiles.shape
    lat, width = queries.shape
    wrow = key_weight.shape[0]
    cols = mine * HD
    tokens = tok * count
    xrow = dx // 4
    any_ = pl.BlockSpec(memory_space=pl.ANY)
    dma = pltpu.SemaphoreType.DMA
    peers = count - 1
    return pl.pallas_call(
        functools.partial(kernel, count=count, mine=mine),
        out_shape=(
            jax.ShapeDtypeStruct((lat // count, width), BF16),
            jax.ShapeDtypeStruct((wrow, width), BF16),
            jax.ShapeDtypeStruct((wrow, width), BF16),
            jax.ShapeDtypeStruct((tok, xrow), BF16),
        ),
        in_specs=[any_] * 5,
        out_specs=(any_, any_, any_, pl.BlockSpec(memory_space=pltpu.VMEM)),
        scratch_shapes=[
            pltpu.VMEM((tokens, dx), BF16),
            pltpu.VMEM((dx, 2 * cols), BF16),
            pltpu.VMEM((lat, cols), BF16),
            pltpu.VMEM((lat, cols), BF16),
            pltpu.VMEM((tokens, 2 * cols), BF16),
            pltpu.VMEM((mine, tokens, lat), F32),
            pltpu.VMEM((mine, tokens, lat), F32),
            pltpu.VMEM((mine, tokens, lat), BF16),
            pltpu.VMEM((tok, lat), BF16),
            pltpu.VMEM((tokens, 2 * cols), BF16),
            pltpu.VMEM((cols, dx), F32),
            pltpu.VMEM((cols, lat), F32),
            pltpu.VMEM((lat, cols), BF16),
            pltpu.VMEM((dx, 2 * cols), BF16),
            pltpu.VMEM((2, count, 2, xrow, tok), BF16),
            pltpu.VMEM((count, 2, xrow, tok), BF16),
            pltpu.VMEM((count, xrow, tok), BF16),
            pltpu.VMEM((count, xrow, tok), BF16),
            pltpu.VMEM((count, xrow, tok), BF16),
            pltpu.VMEM((2, count, xrow, tok), BF16),
            pltpu.VMEM((xrow, tok), F32),
            pltpu.VMEM((mine, 1, lat), F32),
            pltpu.VMEM((mine, 1, lat), F32),
            pltpu.VMEM((mine, 1, lat), F32),
            dma((5,)), dma((3,)),
            dma((2, peers)), dma((2, peers)), dma((peers,)), dma((peers,)),
            dma((2, count)), dma((count,)), dma((count,)), dma((count,)),
            dma((count,)), dma((count,)), dma((count,)), dma((count,)),
            dma((peers,)), dma((peers,)), dma((2, peers)), dma((2, peers)),
            dma((count,)), dma((count,)), dma((count,)), dma((count,)),
            dma((count,)), dma((2, count)),
        ],
        compiler_params=pltpu.CompilerParams(
            collective_id=0, has_side_effects=True, vmem_limit_bytes=60 * 1024 * 1024
        ),
    )(tiles, queries, grad_out, key_weight, value_weight)


def solution(mesh):
    count, groups = mesh.shape["tile"], mesh.shape["head"]

    def body(tiles, queries, grad_out, key_weight, value_weight):
        per = queries.shape[1] // HD
        split = (
            count == 4
            and per % count == 0
            and groups == 4
            and mesh.shape["scan"] == 2
            and tiles.shape[0] % 512 == 0
            and tiles.shape[1] % 64 == 0
            and key_weight.shape[0] % 32 == 0
            and queries.shape[0] % (16 * count) == 0
        )
        chosen = functools.partial(split_body, count, per // count) if split else general_body
        return chosen(tiles, queries, grad_out, key_weight, value_weight)

    placed = (
        P(("scan", "tile"), None),
        P(None, "head"),
        P("scan", "head"),
        P("tile", "head"),
        P("tile", "head"),
    )
    return jax.shard_map(
        body,
        mesh=mesh,
        in_specs=placed,
        out_specs=(
            P(("scan", "tile"), "head"),
            P(("scan", "tile"), "head"),
            P(("scan", "tile"), "head"),
            P(("scan", "tile"), "head"),
        ),
        check_vma=False,
    )
```

```python
import functools

import jax
import jax.numpy as jnp
from jax import lax
from jax.experimental import pallas as pl
from jax.experimental.pallas import tpu as pltpu
from jax.sharding import PartitionSpec as P

HD = 128
MESH = pl.DeviceIdType.MESH
F32 = jnp.float32
BF16 = jnp.bfloat16


def combined_all(part, axis, combine):
    gathered = jax.tree.map(lambda a: lax.all_gather(a, axis), part)

    def take(source):
        return jax.tree.map(lambda a: lax.dynamic_index_in_dim(a, source, 0, False), gathered)

    return lax.fori_loop(
        1, lax.axis_size(axis), lambda source, state: combine(state, take(source)), take(0)
    )


def merge_pair(first, second):
    top = jnp.maximum(first[0], second[0])
    fa = jnp.exp(first[0] - top)
    fb = jnp.exp(second[0] - top)
    return (top, first[1] * fa + second[1] * fb)


def general_body(tiles, queries, grad_out, key_weight, value_weight):
    scale = HD ** (-0.5)
    tok_rows = tiles.shape[0]
    lat_rows = queries.shape[0]
    width = queries.shape[1]
    per = width // HD
    tile_count = lax.axis_size("tile")
    key_full, value_full = (
        lax.all_gather(key_weight, "tile", axis=0, tiled=True),
        lax.all_gather(value_weight, "tile", axis=0, tiled=True),
    )
    keys = jnp.dot(tiles, key_full, preferred_element_type=jnp.float32).astype(jnp.bfloat16)
    values = jnp.dot(tiles, value_full, preferred_element_type=jnp.float32).astype(jnp.bfloat16)
    key_heads = keys.reshape(tok_rows, per, HD)
    value_heads = values.reshape(tok_rows, per, HD)
    query_heads = queries.reshape(lat_rows, per, HD)
    cotangent = grad_out.reshape(lat_rows, per, HD)
    scores = (
        jnp.einsum("qgd,tgd->gqt", query_heads, key_heads, preferred_element_type=jnp.float32)
        * scale
    )
    local_top = jnp.max(scores, axis=-1)
    expo = jnp.exp(scores - local_top[:, :, None])
    local_total = jnp.sum(expo, axis=-1)
    dprobs = jnp.einsum("qgd,tgd->gqt", cotangent, value_heads, preferred_element_type=jnp.float32)
    top, total = combined_all((local_top, local_total), "tile", merge_pair)
    probs = expo * (jnp.exp(local_top - top) / total)[:, :, None]
    probs_b = probs.astype(jnp.bfloat16)
    attn_part = jnp.einsum("gqt,tgd->qgd", probs_b, value_heads, preferred_element_type=jnp.float32)
    attn = lax.psum(attn_part.astype(jnp.bfloat16), "tile").astype(jnp.float32)
    delta = jnp.transpose(jnp.sum(cotangent.astype(jnp.float32) * attn, axis=-1), (1, 0))
    dscores = (probs * (dprobs - delta[:, :, None]) * scale).astype(jnp.bfloat16)
    dkeys = jnp.einsum(
        "gqt,qgd->tgd", dscores, query_heads, preferred_element_type=jnp.float32
    ).astype(jnp.bfloat16)
    dvalues = jnp.einsum(
        "gqt,qgd->tgd", probs_b, cotangent, preferred_element_type=jnp.float32
    ).astype(jnp.bfloat16)
    kv_grad = jnp.concatenate(
        [dkeys.reshape(tok_rows, width), dvalues.reshape(tok_rows, width)], axis=1
    )
    lat_share = lat_rows // tile_count
    block = dscores
    grad_queries = lax.psum_scatter(
        jnp.einsum("gqt,tgd->qgd", block, key_heads, preferred_element_type=jnp.float32)
        .reshape(lat_share * lax.axis_size("tile"), width)
        .astype(jnp.bfloat16),
        "tile",
        scatter_dimension=0,
        tiled=True,
    )
    block = tiles
    both_grads = lax.psum_scatter(
        jnp.einsum("tx,tc->xc", block, kv_grad, preferred_element_type=jnp.float32).astype(
            jnp.bfloat16
        ),
        "tile",
        scatter_dimension=0,
        tiled=True,
    ).astype(jnp.float32)
    grad_key_weight = both_grads[:, :width].astype(jnp.bfloat16)
    grad_value_weight = both_grads[:, width:].astype(jnp.bfloat16)
    stacked = jnp.concatenate([key_full, value_full], axis=1)
    input_term = jnp.einsum("tc,xc->tx", kv_grad, stacked, preferred_element_type=jnp.float32)
    input_term = input_term.astype(jnp.bfloat16).astype(jnp.float32)
    grad_tiles = lax.psum_scatter(
        input_term.astype(jnp.bfloat16), "head", scatter_dimension=1, tiled=True
    )
    return (grad_queries, grad_key_weight, grad_value_weight, grad_tiles)


PIECES = 2


def dot_nn(a, b):
    return lax.dot_general(a, b, (((1,), (0,)), ((), ())), preferred_element_type=F32)


def dot_nt(a, b):
    return lax.dot_general(a, b, (((1,), (1,)), ((), ())), preferred_element_type=F32)


def dot_tn(a, b):
    return lax.dot_general(a, b, (((0,), (0,)), ((), ())), preferred_element_type=F32)


def kernel(
    tiles, queries, grad_out, key_weight, value_weight,
    gq_out, gwk_out, gwv_out, gt_out,
    tf, wc, qs, gs, qt, gt, kv, sc, dp, pb, ds, dkv, acc, dq_acc, gq_buf, gw_buf,
    part, rec_core, snd_x, rec_x, snd_z, rec_z, acc_t, top, total, delta,
    loc_sem, out_sem,
    wz_send, wz_recv, wy_send, wy_recv,
    tz_send, tz_recv, tx_send, tx_recv, tc_send, tc_recv, td_send, td_recv,
    gq_send, gq_recv, gw_send, gw_recv,
    pc_send, pc_recv, px_send, px_recv, pz_send, pz_recv,
    *, count, mine,
):
    scale = HD ** (-0.5)
    scan, t, h = lax.axis_index("scan"), lax.axis_index("tile"), lax.axis_index("head")
    core, chip = lax.rem(h, 2), lax.div(h, 2)
    core_peer = {"head": h + 1 - 2 * core}
    chip_peer = {"head": h + 2 - 4 * chip}
    scan_peer = {"scan": 1 - scan}
    tok = tiles.shape[0]
    lat = queries.shape[0]
    cols = mine * HD
    wrow = key_weight.shape[0]
    half = wrow // 2
    quarter = tok // 4
    lat_own = lat // count
    peers = range(1, count)

    def ahead(k):
        return lax.rem(t + k, count)

    def behind(k):
        return lax.rem(t + count - k, count)

    def at_lanes(index, size):
        return pl.ds(pl.multiple_of(index * size, size), size)

    def rows(start, size, unit):
        return pl.ds(pl.multiple_of(start, unit), size)

    barrier = pltpu.get_barrier_semaphore()
    for k in peers:
        pl.semaphore_signal(barrier, inc=1, device_id={"tile": ahead(k)}, device_id_type=MESH)
    for peer in (core_peer, chip_peer, scan_peer):
        pl.semaphore_signal(barrier, inc=1, device_id=peer, device_id_type=MESH)
    pl.semaphore_wait(barrier, count - 1 + 3)

    def remote(src, dst, send, recv, peer):
        return pltpu.make_async_remote_copy(
            src_ref=src, dst_ref=dst, send_sem=send, recv_sem=recv,
            device_id=peer, device_id_type=MESH,
        )

    def w_send(k, which):
        to = ahead(k)
        src = (key_weight, value_weight)[which].at[rows(scan * half, half, 16), at_lanes(to, cols)]
        dst = wc.at[rows(t * wrow + scan * half, half, 16), pl.ds(which * cols, cols)]
        return remote(src, dst, wz_send.at[which, k - 1], wz_recv.at[which, k - 1], {"tile": to})

    def w_got(k, which):
        piece = wc.at[rows(behind(k) * wrow + scan * half, half, 16), pl.ds(which * cols, cols)]
        return remote(piece, piece, wz_send.at[which, k - 1], wz_recv.at[which, k - 1], scan_peer)

    def w_pass(k):
        piece = wc.at[rows(behind(k) * wrow + scan * half, half, 16), :]
        return remote(piece, piece, wy_send.at[k - 1], wy_recv.at[k - 1], scan_peer)

    def w_passed(k):
        piece = wc.at[rows(behind(k) * wrow + (1 - scan) * half, half, 16), :]
        return remote(piece, piece, wy_send.at[k - 1], wy_recv.at[k - 1], scan_peer)

    part_rows = quarter // PIECES

    def t_piece(source, who, p):
        return tf.at[rows(source * tok + who * quarter + p * part_rows, part_rows, 16), :]

    def t_hop(source, way, p):
        to = {"tile": lax.rem(t + count + 1 - 2 * way, count)}
        piece = t_piece(source, h, p)
        return remote(piece, piece, tz_send.at[way, source, p], tz_recv.at[source, p], to)

    def t_own(way, p):
        to = {"tile": lax.rem(t + count + 1 - 2 * way, count)}
        src = tiles.at[rows(h * quarter + p * part_rows, part_rows, 16), :]
        return remote(src, t_piece(t, h, p), tz_send.at[way, t, p], tz_recv.at[t, p], to)

    def t_move(source, who, send, recv, peer, p):
        piece = t_piece(source, who, p)
        return remote(piece, piece, send.at[source, p], recv.at[source, p], peer)

    inner = (t < count - 1, t > 0)

    def t_stage(j, p):
        for way, source, there in (
            (0, behind(j + 1), t - 1 - j >= 0),
            (1, ahead(j + 1), t + 1 + j < count),
        ):
            @pl.when(there)
            def _(way=way, source=source):
                t_move(source, h, tc_send, tz_recv, core_peer, p).wait_recv()

                @pl.when(inner[way])
                def _():
                    t_hop(source, way, p).start()

                t_move(source, h, tx_send, tx_recv, chip_peer, p).start()
                t_move(source, h, tc_send, tc_recv, core_peer, p).start()

    h_core, h_chip = h + 1 - 2 * core, h + 2 - 4 * chip
    h_diag = h_chip + 1 - 2 * core

    for p in range(PIECES):
        for way in range(2):
            @pl.when(inner[way])
            def _(way=way, p=p):
                t_own(way, p).start()

    for k in peers:
        for which in range(2):
            w_send(k, which).start()
    local = [
        pltpu.make_async_copy(tiles, tf.at[rows(t * tok, tok, 16), :], loc_sem.at[0]),
        pltpu.make_async_copy(
            key_weight.at[:, at_lanes(t, cols)], wc.at[rows(t * wrow, wrow, 16), pl.ds(0, cols)],
            loc_sem.at[1],
        ),
        pltpu.make_async_copy(
            value_weight.at[:, at_lanes(t, cols)],
            wc.at[rows(t * wrow, wrow, 16), pl.ds(cols, cols)], loc_sem.at[2],
        ),
        pltpu.make_async_copy(queries.at[:, at_lanes(t, cols)], qs, loc_sem.at[3]),
        pltpu.make_async_copy(grad_out.at[:, at_lanes(t, cols)], gs, loc_sem.at[4]),
    ]
    for copy in local:
        copy.start()
    top[...] = jnp.full_like(top, -jnp.inf)
    for copy in local:
        copy.wait()
    qt[...] = jnp.transpose(qs[...], (1, 0))
    gt[...] = jnp.transpose(gs[...], (1, 0))
    for p in range(PIECES):
        t_stage(0, p)
    for k in peers:
        for which in range(2):
            w_got(k, which).wait_recv()
        w_pass(k).start()
    for j in range(1, count - 1):
        for p in range(PIECES):
            t_stage(j, p)
    for k in peers:
        w_passed(k).wait_recv()

    SUB = 512

    def project(block):
        def sub(i, carry):
            at = rows(block * tok + i * SUB, SUB, SUB)
            kv[at, :] = dot_nn(tf[at, :], wc[...]).astype(BF16)
            for m in range(mine):
                lanes = slice(m * HD, (m + 1) * HD)
                vlanes = slice(cols + m * HD, cols + (m + 1) * HD)
                score = dot_nn(kv[at, lanes], qt[lanes, :]) * scale
                sc[m, at, :] = score
                top[m, :, :] = jnp.maximum(top[m, :, :], jnp.max(score, axis=0, keepdims=True))
                dp[m, at, :] = dot_nn(kv[at, vlanes], gt[lanes, :])
            return carry

        lax.fori_loop(0, tok // SUB, sub, 0)

    def chip_stage(j):
        for source, there in ((behind(j + 1), t - 1 - j >= 0), (ahead(j + 1), t + 1 + j < count)):
            @pl.when(there)
            def _(source=source):
                for p in range(PIECES):
                    t_move(source, h_chip, tx_send, tx_recv, chip_peer, p).wait_recv()
                    t_move(source, h_chip, td_send, td_recv, core_peer, p).start()

    def block_stage(j, carry):
        chip_stage(j)
        for source, there in (
            (lax.rem(t + count - 1 - j, count), t - 1 - j >= 0),
            (lax.rem(t + 1 + j, count), t + 1 + j < count),
        ):
            @pl.when(there)
            def _(source=source):
                for p in range(PIECES):
                    t_move(source, h_core, tc_send, tc_recv, core_peer, p).wait_recv()
                    t_move(source, h_diag, td_send, td_recv, core_peer, p).wait_recv()
                project(source)
        return carry

    project(t)
    lax.fori_loop(0, count - 1, block_stage, 0)

    total[...] = jnp.zeros_like(total)

    EL = 128

    def exps(i, carry):
        at = rows(i * EL, EL, EL)
        for m in range(mine):
            expo = jnp.exp(sc[m, at, :] - top[m, :, :])
            sc[m, at, :] = expo
            total[m, :, :] = total[m, :, :] + jnp.sum(expo, axis=0, keepdims=True)
        return carry

    lax.fori_loop(0, count * tok // EL, exps, 0)
    total[...] = 1.0 / total[...]
    delta[...] = jnp.zeros_like(delta)

    def probs(i, carry):
        at = rows(i * EL, EL, EL)
        for m in range(mine):
            prob = sc[m, at, :] * total[m, :, :]
            prob_b = prob.astype(BF16)
            sc[m, at, :] = prob
            pb[m, at, :] = prob_b
            delta[m, :, :] = delta[m, :, :] + jnp.sum(
                prob_b.astype(F32) * dp[m, at, :], axis=0, keepdims=True
            )
        return carry

    lax.fori_loop(0, count * tok // EL, probs, 0)

    def weight_grad(lo):
        acc[...] = jnp.zeros_like(acc)

        def block(b, carry):
            at = rows(b * tok, tok, tok)
            term = dot_tn(dkv[at, lo : lo + cols], tf[at, :])
            acc[...] += term.astype(BF16).astype(F32)
            return carry

        lax.fori_loop(0, count, block, 0)
        gw_buf[:, lo : lo + cols] = jnp.transpose(acc[...], (1, 0)).astype(BF16)

    def gw_own(which):
        out = (gwk_out, gwv_out)[which]
        return pltpu.make_async_copy(
            gw_buf.at[rows(t * wrow, wrow, 16), pl.ds(which * cols, cols)],
            out.at[:, at_lanes(t, cols)], out_sem.at[which],
        )

    def gw_move(k, which):
        out = (gwk_out, gwv_out)[which]
        to = ahead(k)
        return remote(
            gw_buf.at[rows(to * wrow, wrow, 16), pl.ds(which * cols, cols)],
            out.at[:, at_lanes(t, cols)],
            gw_send.at[which, k - 1], gw_recv.at[which, k - 1], {"tile": to},
        )

    def gw_got(k, which):
        out = (gwk_out, gwv_out)[which]
        return remote(
            gw_buf.at[rows(t * wrow, wrow, 16), pl.ds(which * cols, cols)],
            out.at[:, at_lanes(behind(k), cols)],
            gw_send.at[which, k - 1], gw_recv.at[which, k - 1], {"tile": ahead(k)},
        )

    def dvals(b, carry):
        at = rows(b * tok, tok, tok)
        for m in range(mine):
            lanes = slice(m * HD, (m + 1) * HD)
            dkv[at, cols + m * HD : cols + (m + 1) * HD] = dot_nn(
                pb[m, at, :], gs[:, lanes]
            ).astype(BF16)
        return carry

    lax.fori_loop(0, count, dvals, 0)
    weight_grad(cols)
    for k in peers:
        gw_move(k, 1).start()
    gw_own(1).start()

    dq_acc[...] = jnp.zeros_like(dq_acc)

    def part_core(b):
        return remote(
            part.at[1 - core, b], rec_core.at[b], pc_send.at[b], pc_recv.at[b], core_peer
        )

    xrow = tiles.shape[1] // 4

    def order(j):
        low = lax.rem(t, 2)
        high = lax.div(t, 2)
        first, second, third = 3 - 3 * high, 2 - 2 * low + high, 1 + low
        return jnp.where(j == 0, first, jnp.where(j == 1, second, jnp.where(j == 2, third, t)))

    def part_chip(b):
        return remote(snd_x.at[b], rec_x.at[b], px_send.at[b], px_recv.at[b], chip_peer)

    def to_chip(b):
        part_core(b).wait_recv()
        snd_x[b, :, :] = (
            part[core, b, 1 - chip, :, :].astype(F32) + rec_core[b, 1 - chip, :, :].astype(F32)
        ).astype(BF16)
        part_chip(b).start()

    def grads(j, carry):
        b = order(j)
        at = rows(b * tok, tok, tok)
        for m in range(mine):
            lanes = slice(m * HD, (m + 1) * HD)

            def sub(i, carry):
                sub_at = rows(b * tok + i * EL, EL, EL)
                ds[pl.ds(pl.multiple_of(i * EL, EL), EL), :] = (
                    sc[m, sub_at, :] * (dp[m, sub_at, :] - delta[m, :, :]) * scale
                ).astype(BF16)
                return carry

            lax.fori_loop(0, tok // EL, sub, 0)
            dkv[at, lanes] = dot_nn(ds[...], qs[:, lanes]).astype(BF16)
            dq_acc[lanes, :] += dot_tn(kv[at, lanes], ds[...]).astype(BF16).astype(F32)
        for group in range(4):
            part[group % 2, b, group // 2, :, :] = dot_nt(
                wc[group * xrow : (group + 1) * xrow, :], dkv[at, :]
            ).astype(BF16)
        part_core(b).start()

        @pl.when(j > 0)
        def _():
            to_chip(order(j - 1))

        return carry

    lax.fori_loop(0, count, grads, 0)
    to_chip(order(count - 1))
    gq_buf[...] = jnp.transpose(dq_acc[...], (1, 0)).astype(BF16)

    def gq_move(k):
        return remote(
            gq_buf.at[rows(ahead(k) * lat_own, lat_own, 16), :], gq_out.at[:, at_lanes(t, cols)],
            gq_send.at[k - 1], gq_recv.at[k - 1], {"tile": ahead(k)},
        )

    def gq_got(k):
        return remote(
            gq_buf.at[rows(t * lat_own, lat_own, 16), :],
            gq_out.at[:, at_lanes(behind(k), cols)],
            gq_send.at[k - 1], gq_recv.at[k - 1], {"tile": ahead(k)},
        )

    gq_own = pltpu.make_async_copy(
        gq_buf.at[rows(t * lat_own, lat_own, 16), :], gq_out.at[:, at_lanes(t, cols)],
        out_sem.at[2],
    )

    for k in peers:
        gq_move(k).start()
    gq_own.start()
    weight_grad(0)
    for k in peers:
        gw_move(k, 0).start()
    gw_own(0).start()

    def summed(b):
        return (
            part[core, b, chip, :, :].astype(F32)
            + rec_core[b, chip, :, :].astype(F32)
            + rec_x[b, :, :].astype(F32)
        )

    def part_tile(b, way):
        to = {"tile": lax.rem(t + count + 1 - 2 * way, count)}
        return remote(
            snd_z.at[b], rec_z.at[way, b], pz_send.at[b], pz_recv.at[way, b], to
        )

    for j in range(count - 1):
        b = order(j)
        part_chip(b).wait_recv()
        for way, onward, fed in ((0, b > t, t > 0), (1, b < t, t < count - 1)):
            @pl.when(onward)
            def _(way=way, fed=fed, b=b):
                @pl.when(fed)
                def _():
                    part_tile(b, way).wait_recv()
                    snd_z[b, :, :] = (summed(b) + rec_z[way, b, :, :].astype(F32)).astype(BF16)

                @pl.when(jnp.logical_not(fed))
                def _():
                    snd_z[b, :, :] = summed(b).astype(BF16)

                part_tile(b, way).start()

    part_chip(t).wait_recv()
    acc_t[...] = summed(t)
    for way, fed in ((0, t > 0), (1, t < count - 1)):
        @pl.when(fed)
        def _(way=way):
            part_tile(t, way).wait_recv()
            acc_t[...] += rec_z[way, t, :, :].astype(F32)

    gt_out[...] = jnp.transpose(acc_t[...], (1, 0)).astype(BF16)

    for k in peers:
        for which in range(2):
            w_send(k, which).wait_send()
            gw_got(k, which).wait_recv()
            gw_move(k, which).wait_send()
        w_pass(k).wait_send()
        source = behind(k)
        for p in range(PIECES):
            t_move(source, h, tx_send, tx_recv, chip_peer, p).wait_send()
            t_move(source, h, tc_send, tc_recv, core_peer, p).wait_send()
            t_move(source, h_chip, td_send, td_recv, core_peer, p).wait_send()
        gq_got(k).wait_recv()
        gq_move(k).wait_send()
        part_tile(behind(k), 0).wait_send()
    for way in range(2):
        @pl.when(inner[way])
        def _(way=way):
            for p in range(PIECES):
                t_own(way, p).wait_send()
            for j in range(count - 1):
                source = (behind, ahead)[way](j + 1)

                @pl.when((t - 1 - j >= 0, t + 1 + j < count)[way])
                def _():
                    for p in range(PIECES):
                        t_hop(source, way, p).wait_send()

    for j in range(count):
        part_core(j).wait_send()
        part_chip(j).wait_send()
    gq_own.wait()
    gw_own(0).wait()
    gw_own(1).wait()


def split_body(count, mine, tiles, queries, grad_out, key_weight, value_weight):
    tok, dx = tiles.shape
    lat, width = queries.shape
    wrow = key_weight.shape[0]
    cols = mine * HD
    tokens = tok * count
    xrow = dx // 4
    any_ = pl.BlockSpec(memory_space=pl.ANY)
    dma = pltpu.SemaphoreType.DMA
    peers = count - 1
    return pl.pallas_call(
        functools.partial(kernel, count=count, mine=mine),
        out_shape=(
            jax.ShapeDtypeStruct((lat // count, width), BF16),
            jax.ShapeDtypeStruct((wrow, width), BF16),
            jax.ShapeDtypeStruct((wrow, width), BF16),
            jax.ShapeDtypeStruct((tok, xrow), BF16),
        ),
        in_specs=[any_] * 5,
        out_specs=(any_, any_, any_, pl.BlockSpec(memory_space=pltpu.VMEM)),
        scratch_shapes=[
            pltpu.VMEM((tokens, dx), BF16),
            pltpu.VMEM((dx, 2 * cols), BF16),
            pltpu.VMEM((lat, cols), BF16),
            pltpu.VMEM((lat, cols), BF16),
            pltpu.VMEM((cols, lat), BF16),
            pltpu.VMEM((cols, lat), BF16),
            pltpu.VMEM((tokens, 2 * cols), BF16),
            pltpu.VMEM((mine, tokens, lat), F32),
            pltpu.VMEM((mine, tokens, lat), F32),
            pltpu.VMEM((mine, tokens, lat), BF16),
            pltpu.VMEM((tok, lat), BF16),
            pltpu.VMEM((tokens, 2 * cols), BF16),
            pltpu.VMEM((cols, dx), F32),
            pltpu.VMEM((cols, lat), F32),
            pltpu.VMEM((lat, cols), BF16),
            pltpu.VMEM((dx, 2 * cols), BF16),
            pltpu.VMEM((2, count, 2, xrow, tok), BF16),
            pltpu.VMEM((count, 2, xrow, tok), BF16),
            pltpu.VMEM((count, xrow, tok), BF16),
            pltpu.VMEM((count, xrow, tok), BF16),
            pltpu.VMEM((count, xrow, tok), BF16),
            pltpu.VMEM((2, count, xrow, tok), BF16),
            pltpu.VMEM((xrow, tok), F32),
            pltpu.VMEM((mine, 1, lat), F32),
            pltpu.VMEM((mine, 1, lat), F32),
            pltpu.VMEM((mine, 1, lat), F32),
            dma((5,)), dma((3,)),
            dma((2, peers)), dma((2, peers)), dma((peers,)), dma((peers,)),
            dma((2, count, PIECES)), dma((count, PIECES)), dma((count, PIECES)), dma((count, PIECES)),
            dma((count, PIECES)), dma((count, PIECES)), dma((count, PIECES)), dma((count, PIECES)),
            dma((peers,)), dma((peers,)), dma((2, peers)), dma((2, peers)),
            dma((count,)), dma((count,)), dma((count,)), dma((count,)),
            dma((count,)), dma((2, count)),
        ],
        compiler_params=pltpu.CompilerParams(
            collective_id=0, has_side_effects=True, vmem_limit_bytes=60 * 1024 * 1024
        ),
    )(tiles, queries, grad_out, key_weight, value_weight)


def solution(mesh):
    count, groups = mesh.shape["tile"], mesh.shape["head"]

    def body(tiles, queries, grad_out, key_weight, value_weight):
        per = queries.shape[1] // HD
        split = (
            count == 4
            and per % count == 0
            and groups == 4
            and mesh.shape["scan"] == 2
            and tiles.shape[0] % 512 == 0
            and tiles.shape[1] % 64 == 0
            and key_weight.shape[0] % 32 == 0
            and queries.shape[0] % (16 * count) == 0
        )
        chosen = functools.partial(split_body, count, per // count) if split else general_body
        return chosen(tiles, queries, grad_out, key_weight, value_weight)

    placed = (
        P(("scan", "tile"), None),
        P(None, "head"),
        P("scan", "head"),
        P("tile", "head"),
        P("tile", "head"),
    )
    return jax.shard_map(
        body,
        mesh=mesh,
        in_specs=placed,
        out_specs=(
            P(("scan", "tile"), "head"),
            P(("scan", "tile"), "head"),
            P(("scan", "tile"), "head"),
            P(("scan", "tile"), "head"),
        ),
        check_vma=False,
    )
```
